32 devices in a mesh: grp: 1, dev: 32 (over z, y, x, core).
Axes of the slice: x: 2, y: 2, z: 4, core: 2. Of those that a mesh axis runs over, the one named last changes fastest.
Arguments:
- hidden_in: bfloat16 [640, 32, 768], P(('grp', 'dev')), may hold values from -6 to 6
- grad_out: bfloat16 [640, 32, 768], P(('grp', 'dev')), may hold values from -6 to 6
- norm_gain: float32 [768], replicated, may hold values from 0.25 to 1.75
- w_qkv: bfloat16 [768, 2304], replicated, may hold values from -0.21875 to 0.21875
- w_out: bfloat16 [768, 768], replicated, may hold values from -0.21875 to 0.21875
- sharpness: float32 [12], replicated, may hold values from 4 to 20
- cohort_ids: int32 [640], P('grp'), may hold values from 0 to 3
- observed: int32 [640, 32], P('grp', 'dev'), may hold values 0 or 1
Outputs:
- grad_in: bfloat16 [640, 32, 768], P(('grp', 'dev'))
- grad_qkv: float32 [768, 2304], P(('grp', 'dev'))
- grad_wout: float32 [768, 768], P(('grp', 'dev'))
The draws below stay inside these ranges and needn't reach their ends.
All inputs are finite; a program needn't handle non-finite values. No bound on the sum of `observed` on one device may be relied on, other than what follows from the above.
Results may differ from the reference program's by a relative error of at most 0.015.
Values may be sent and summed in bfloat16 or wider, within the bound.
A program may use at most 128 MiB of HBM per device.

```python
import math
import jax
import jax.numpy as jnp
from jax import lax

D = 768
H = 12
COHORTS = 4
C = 640
P_SIZE = 32
N_DEV = 32


def touch_ends(values, key, least, largest):
    spot = [jax.random.randint(jax.random.fold_in(key, axis), (), 0, length) for axis, length in enumerate(values.shape)]
    longest = values.shape.index(max(values.shape))
    next_to = spot[:longest] + [(spot[longest] + 1) % values.shape[longest]] + spot[longest + 1:]
    return values.at[tuple(spot)].set(least).at[tuple(next_to)].set(largest)


def steps_of(stream_key, extent, split, least, largest):
    loudness, own = 1.0, jax.random.fold_in(stream_key, 6)
    for axis_at, parts in split:
        draws = jnp.exp(jax.random.uniform(jax.random.fold_in(own, axis_at), (parts,), jnp.float32, least / len(split), largest / len(split)))
        loudness = loudness * jnp.repeat(draws, extent[axis_at] // parts).reshape([-1 if axis == axis_at else 1 for axis in range(len(extent))])
    return loudness


def noise(stream_key, shape, deviation, bound, cuts=(), kind=jnp.bfloat16):
    factor_of = steps_of(stream_key, shape, cuts, -0.22, 0.18) if cuts else 1.0
    array = jax.random.normal(stream_key, shape, jnp.float32) * deviation * factor_of
    return jnp.minimum(jnp.maximum(array, -bound), bound).astype(kind)


def setup_inputs(seed: int = 0, part: int = 0) -> dict:
    key_list = jax.random.split(jax.random.key(seed), 9)
    own_keys = jax.random.split(jax.random.fold_in(key_list[8], part), 9)
    hidden_in = noise(own_keys[0], (C, P_SIZE, D), 1.0, 6.0, ((0, 32),))
    grad_out = noise(own_keys[1], (C, P_SIZE, D), 1.0, 6.0, ((0, 32),))
    norm_gain = jnp.clip(1.0 + 0.15 * jax.random.normal(key_list[2], (D,), jnp.float32), 0.25, 1.75)
    w_qkv = noise(key_list[3], (D, 3 * D), D ** -0.5, 0.21875)
    w_out = noise(key_list[4], (D, D), D ** -0.5, 0.21875)
    sharpness = jnp.clip(jnp.exp(jax.random.uniform(key_list[5], (H,), jnp.float32, math.log(4.0), math.log(20.0))), 4.0, 20.0)
    cohort_ids = touch_ends(jax.random.randint(own_keys[6], (C,), 0, COHORTS), jax.random.fold_in(own_keys[6], 1), 0, COHORTS - 1).astype(jnp.int32)
    observed = touch_ends((jax.random.randint(own_keys[7], (C, P_SIZE), 0, 4) < 3).astype(jnp.int32), jax.random.fold_in(own_keys[7], 1), 0, 1)
    return dict(hidden_in=hidden_in, grad_out=grad_out, norm_gain=norm_gain, w_qkv=w_qkv, w_out=w_out, sharpness=sharpness, cohort_ids=cohort_ids, observed=observed)


epsilon = 1e-06

def block_grads(rows_in, grad_rows, observed_block, norm_gain, w_qkv, w_out, sharpness, cohort_ids):
    campaigns, patches, width = rows_in.shape
    heads = sharpness.shape[0]
    head_size = width // heads
    values = rows_in.astype(jnp.float32)
    inv_rms = lax.rsqrt(lax.optimization_barrier(jnp.mean(values * values, axis=-1, keepdims=True)) + epsilon)
    unit_rows = values * inv_rms
    normed = (unit_rows * norm_gain).astype(jnp.bfloat16).reshape(-1, width)
    projected = jnp.dot(normed, w_qkv, preferred_element_type=jnp.float32)
    shape4 = (campaigns, patches, heads, head_size)
    query_raw = projected[:, :width].reshape(shape4)
    key_raw = projected[:, width:2 * width].reshape(shape4)
    value_raw = projected[:, 2 * width:].reshape(shape4)
    query_inv = lax.rsqrt(lax.optimization_barrier(jnp.mean(query_raw * query_raw, axis=-1, keepdims=True)) + epsilon)
    key_inv = lax.rsqrt(lax.optimization_barrier(jnp.mean(key_raw * key_raw, axis=-1, keepdims=True)) + epsilon)
    query_unit = query_raw * query_inv
    key_unit = key_raw * key_inv
    query_half = query_unit.astype(jnp.bfloat16).astype(jnp.float32)
    key_half = key_unit.astype(jnp.bfloat16).astype(jnp.float32)
    value_half = value_raw.astype(jnp.bfloat16).astype(jnp.float32)
    dy_rows = grad_rows.reshape(-1, width)
    grad_attn = lax.dot_general(dy_rows, w_out, (((1,), (1,)), ((), ())), preferred_element_type=jnp.float32)
    grad_attn = grad_attn.astype(jnp.bfloat16).astype(jnp.float32).reshape(shape4)
    same = cohort_ids[:, None] == cohort_ids[None, :]
    diagonal = jnp.eye(campaigns, dtype=bool)
    keys_seen = (observed_block.T == 1)[:, None, :]
    allowed = jnp.where(same[None] & (keys_seen | diagonal[None]), 1.0, 0.0).astype(jnp.float32)
    scale = (sharpness / head_size)[:, None, None, None]
    scores = jnp.einsum('iphe,jphe->hpij', query_half, key_half) * scale
    raw_weights = jnp.exp(scores) * allowed[None]
    probs = raw_weights / lax.optimization_barrier(jnp.sum(raw_weights, axis=-1, keepdims=True))
    probs_half = probs.astype(jnp.bfloat16).astype(jnp.float32)
    attended = jnp.einsum('hpij,jphe->iphe', probs_half, value_half)
    grad_probs = jnp.einsum('iphe,jphe->hpij', grad_attn, value_half)
    grad_value = jnp.einsum('hpij,iphe->jphe', probs_half, grad_attn)
    row_dot = lax.optimization_barrier(jnp.sum(grad_probs * probs, axis=-1, keepdims=True))
    grad_scores = (probs * (grad_probs - row_dot) * scale).astype(jnp.bfloat16).astype(jnp.float32)
    grad_qunit = jnp.einsum('hpij,jphe->iphe', grad_scores, key_half)
    grad_kunit = jnp.einsum('hpij,iphe->jphe', grad_scores, query_half)
    grad_query = query_inv * (grad_qunit - query_unit * lax.optimization_barrier(jnp.mean(grad_qunit * query_unit, axis=-1, keepdims=True)))
    grad_key = key_inv * (grad_kunit - key_unit * lax.optimization_barrier(jnp.mean(grad_kunit * key_unit, axis=-1, keepdims=True)))
    grad_proj = jnp.concatenate([grad_query.reshape(-1, width), grad_key.reshape(-1, width), grad_value.reshape(-1, width)], axis=1).astype(jnp.bfloat16)
    attended_half = attended.astype(jnp.bfloat16).reshape(-1, width)
    out_term = lax.dot_general(attended_half, dy_rows, (((0,), (0,)), ((), ())), preferred_element_type=jnp.float32)
    qkv_term = lax.dot_general(normed, grad_proj, (((0,), (0,)), ((), ())), preferred_element_type=jnp.float32)
    grad_normed = lax.dot_general(grad_proj, w_qkv, (((1,), (1,)), ((), ())), preferred_element_type=jnp.float32)
    shaped = grad_normed.reshape(campaigns, patches, width) * norm_gain
    result = grad_rows.astype(jnp.float32) + inv_rms * (shaped - unit_rows * lax.optimization_barrier(jnp.mean(shaped * unit_rows, axis=-1, keepdims=True)))
    return (result.astype(jnp.bfloat16), qkv_term, out_term)

def reference(hidden_in, grad_out, norm_gain, w_qkv, w_out, sharpness, cohort_ids, observed):
    campaigns, patches, width = hidden_in.shape
    per_block = patches // N_DEV

    def step(carry, block):
        start = (block * per_block).astype(jnp.int32)
        rows_in = lax.dynamic_slice_in_dim(hidden_in, start, per_block, 1)
        grad_rows = lax.dynamic_slice_in_dim(grad_out, start, per_block, 1)
        observed_block = lax.dynamic_slice_in_dim(observed, start, per_block, 1)
        result, qkv_term, out_term = block_grads(rows_in, grad_rows, observed_block, norm_gain, w_qkv, w_out, sharpness, cohort_ids)
        qkv_round = lax.optimization_barrier(qkv_term.astype(jnp.bfloat16)).astype(jnp.float32)
        out_round = lax.optimization_barrier(out_term.astype(jnp.bfloat16)).astype(jnp.float32)
        return ((carry[0] + qkv_round, carry[1] + out_round), result)
    start_sums = (jnp.zeros((width, 3 * width), jnp.float32), jnp.zeros((width, width), jnp.float32))
    sums, results = lax.scan(step, start_sums, jnp.arange(N_DEV, dtype=jnp.int32))
    grad_in = jnp.moveaxis(results, 0, 1).reshape(campaigns, patches, width)
    return (grad_in, sums[0], sums[1])
```

```python
import functools
import math

import jax
import jax.numpy as jnp
from jax import lax
from jax.experimental import pallas as pl
from jax.experimental.pallas import tpu as pltpu
from jax.sharding import PartitionSpec as P

epsilon = 1e-06
log2e = math.log2(math.e)


def dot(left, right, dims):
    return lax.dot_general(left, right, ((dims[0], dims[1]), ((), ())), preferred_element_type=jnp.float32)


def compute_kernel(
    head_size,
    group,
    sharp_ref,
    x_ref,
    dy_ref,
    gain_ref,
    wq_ref,
    wk_ref,
    wv_ref,
    wo_ref,
    cohort_col_ref,
    cohort_row_ref,
    seen_ref,
    gin_ref,
    gqkv_ref,
    gwo_ref,
    normed_ref,
    normed_t_ref,
    mask_ref,
    acc_ref,
    dproj_ref,
    att_ref,
):
    step = pl.program_id(0)
    rows, width = x_ref.shape
    gw = group * head_size

    @pl.when(step == 0)
    def _():
        values = x_ref[...].astype(jnp.float32)
        inv = lax.rsqrt(jnp.mean(values * values, axis=-1, keepdims=True) + epsilon)
        normed = values * inv * gain_ref[...]
        normed_ref[...] = normed.astype(jnp.bfloat16)
        normed_t_ref[...] = normed.T.astype(jnp.bfloat16)
        same = cohort_col_ref[...] == cohort_row_ref[...]
        diagonal = lax.broadcasted_iota(jnp.int32, (rows, rows), 0) == lax.broadcasted_iota(
            jnp.int32, (rows, rows), 1
        )
        seen = jnp.broadcast_to(seen_ref[...], (rows, rows)) == 1
        mask_ref[...] = jnp.where(same & (seen | diagonal), 1.0, 0.0)
        acc_ref[...] = jnp.zeros_like(acc_ref)

    normed = normed_ref[...]
    q_raw = dot(normed, wq_ref[...], ((1,), (0,)))
    k_raw = dot(normed, wk_ref[...], ((1,), (0,)))
    v_half = dot(normed, wv_ref[...], ((1,), (0,))).astype(jnp.bfloat16)
    da_half = dot(dy_ref[...], wo_ref[...], ((1,), (1,))).astype(jnp.bfloat16)
    for h in range(group):
        lanes = slice(h * head_size, (h + 1) * head_size)
        q = q_raw[:, lanes]
        k = k_raw[:, lanes]
        v = v_half[:, lanes]
        da = da_half[:, lanes]
        q_inv = lax.rsqrt(jnp.mean(q * q, axis=-1, keepdims=True) + epsilon)
        k_inv = lax.rsqrt(jnp.mean(k * k, axis=-1, keepdims=True) + epsilon)
        q_unit = q * q_inv
        k_unit = k * k_inv
        q_half = q_unit.astype(jnp.bfloat16)
        k_half = k_unit.astype(jnp.bfloat16)
        k_t = k_unit.T.astype(jnp.bfloat16)
        v_t = v.astype(jnp.float32).T.astype(jnp.bfloat16)
        scale = sharp_ref[step * group + h] / head_size
        scores = dot(k_half, q_half, ((1,), (1,)))
        grad_probs = dot(v, da, ((1,), (1,)))
        weights = jnp.exp2(scores * (scale * log2e)) * mask_ref[...]
        probs = weights * (1.0 / jnp.sum(weights, axis=0, keepdims=True))
        probs_half = probs.astype(jnp.bfloat16)
        att_t = dot(v_t, probs_half, ((1,), (0,)))
        grad_v = dot(probs_half, da, ((1,), (0,)))
        row_dot = jnp.sum(grad_probs * probs, axis=0, keepdims=True)
        grad_scores = (probs * (grad_probs - row_dot)).astype(jnp.bfloat16)
        dq = dot(k_t, grad_scores, ((1,), (0,))).T * scale
        dk = dot(grad_scores, q_half, ((1,), (0,))) * scale
        dq = q_inv * (dq - q_unit * jnp.mean(dq * q_unit, axis=-1, keepdims=True))
        dk = k_inv * (dk - k_unit * jnp.mean(dk * k_unit, axis=-1, keepdims=True))
        base = h * head_size
        dproj_ref[:, base : base + head_size] = dq.astype(jnp.bfloat16)
        dproj_ref[:, gw + base : gw + base + head_size] = dk.astype(jnp.bfloat16)
        dproj_ref[:, 2 * gw + base : 2 * gw + base + head_size] = grad_v.astype(jnp.bfloat16)
        att_ref[base : base + head_size, :] = att_t.astype(jnp.bfloat16)
    gwo_ref[...] = dot(att_ref[...], dy_ref[...], ((1,), (0,))).astype(jnp.bfloat16)
    gqkv_ref[0] = dot(normed_t_ref[...], dproj_ref[...], ((1,), (0,))).astype(jnp.bfloat16)
    acc_ref[...] += (
        dot(dproj_ref[:, :gw], wq_ref[...], ((1,), (1,)))
        + dot(dproj_ref[:, gw : 2 * gw], wk_ref[...], ((1,), (1,)))
        + dot(dproj_ref[:, 2 * gw :], wv_ref[...], ((1,), (1,)))
    )

    @pl.when(step == pl.num_programs(0) - 1)
    def _():
        values = x_ref[...].astype(jnp.float32)
        inv = lax.rsqrt(jnp.mean(values * values, axis=-1, keepdims=True) + epsilon)
        unit = values * inv
        shaped = acc_ref[...] * gain_ref[...]
        result = dy_ref[...].astype(jnp.float32) + inv * (
            shaped - unit * jnp.mean(shaped * unit, axis=-1, keepdims=True)
        )
        gin_ref[...] = result.astype(jnp.bfloat16)


def patch_grads(x, dy, norm_gain, w_qkv, w_out, sharpness, cohort_ids, seen):
    rows, width = x.shape
    heads = sharpness.shape[0]
    head_size = width // heads
    group = math.gcd(heads, 2)
    steps = heads // group
    gw = group * head_size
    whole = lambda shape: pl.BlockSpec(shape, lambda g: (0,) * len(shape))
    return pl.pallas_call(
        functools.partial(compute_kernel, head_size, group),
        grid=(steps,),
        in_specs=[
            pl.BlockSpec(memory_space=pltpu.SMEM),
            whole((rows, width)),
            whole((rows, width)),
            whole((1, width)),
            pl.BlockSpec((width, gw), lambda g: (0, g)),
            pl.BlockSpec((width, gw), lambda g: (0, steps + g)),
            pl.BlockSpec((width, gw), lambda g: (0, 2 * steps + g)),
            pl.BlockSpec((gw, width), lambda g: (g, 0)),
            whole((rows, 1)),
            whole((1, rows)),
            whole((rows, 1)),
        ],
        out_specs=[
            whole((rows, width)),
            pl.BlockSpec((1, width, 3 * gw), lambda g: (g, 0, 0)),
            pl.BlockSpec((gw, width), lambda g: (g, 0)),
        ],
        out_shape=[
            jax.ShapeDtypeStruct((rows, width), jnp.bfloat16),
            jax.ShapeDtypeStruct((steps, width, 3 * gw), jnp.bfloat16),
            jax.ShapeDtypeStruct((width, width), jnp.bfloat16),
        ],
        scratch_shapes=[
            pltpu.VMEM((rows, width), jnp.bfloat16),
            pltpu.VMEM((width, rows), jnp.bfloat16),
            pltpu.VMEM((rows, rows), jnp.float32),
            pltpu.VMEM((rows, width), jnp.float32),
            pltpu.VMEM((rows, 3 * gw), jnp.bfloat16),
            pltpu.VMEM((gw, rows), jnp.bfloat16),
        ],
        compiler_params=pltpu.CompilerParams(vmem_limit_bytes=60 * 1024 * 1024),
    )(
        sharpness,
        x,
        dy,
        norm_gain[None, :],
        w_qkv,
        w_qkv,
        w_qkv,
        w_out,
        cohort_ids[:, None],
        cohort_ids[None, :],
        seen,
    )


def body(hidden_in, grad_out, norm_gain, w_qkv, w_out, sharpness, cohort_ids, observed):
    width = hidden_in.shape[-1]
    heads = sharpness.shape[0]
    x = lax.all_to_all(hidden_in, "dev", split_axis=1, concat_axis=0, tiled=True)
    dy = lax.all_to_all(grad_out, "dev", split_axis=1, concat_axis=0, tiled=True)
    campaigns, patches, _ = x.shape
    gin, gqkv, gwo = [], 0.0, 0.0
    for p in range(patches):
        a, b, c = patch_grads(
            x[:, p], dy[:, p], norm_gain, w_qkv, w_out, sharpness, cohort_ids, observed[:, p : p + 1]
        )
        gin.append(a)
        gqkv, gwo = (b, c) if p == 0 else (gqkv + b, gwo + c)
    grad_in = lax.all_to_all(
        jnp.stack(gin, axis=1), "dev", split_axis=0, concat_axis=1, tiled=True
    )
    steps = gqkv.shape[0]
    gqkv = lax.psum_scatter(gqkv, "dev", scatter_dimension=1, tiled=True)
    gwo = lax.psum_scatter(gwo, "dev", scatter_dimension=0, tiled=True)
    part = gqkv.shape[1]
    gqkv = gqkv.reshape(steps, part, 3, width // steps).transpose(1, 2, 0, 3).reshape(part, 3 * width)
    return (grad_in, gqkv.astype(jnp.float32), gwo.astype(jnp.float32))


def solution(mesh):
    in_specs = (
        P(("grp", "dev"), None, None),
        P(("grp", "dev"), None, None),
        P(),
        P(),
        P(),
        P(),
        P("grp"),
        P("grp", "dev"),
    )
    out_specs = (P(("grp", "dev"), None, None), P(("grp", "dev"), None), P(("grp", "dev"), None))
    return jax.shard_map(body, mesh=mesh, in_specs=in_specs, out_specs=out_specs, check_vma=False)
```

```python
import functools
import math

import jax
import jax.numpy as jnp
from jax import lax
from jax.experimental import pallas as pl
from jax.experimental.pallas import tpu as pltpu
from jax.sharding import PartitionSpec as P

epsilon = 1e-06
log2e = math.log2(math.e)


def dot(left, right, dims):
    return lax.dot_general(left, right, ((dims[0], dims[1]), ((), ())), preferred_element_type=jnp.float32)


def compute_kernel(
    head_size,
    group,
    sharp_ref,
    x_ref,
    dy_ref,
    gain_ref,
    wq_ref,
    wk_ref,
    wv_ref,
    wo_ref,
    cohort_col_ref,
    cohort_row_ref,
    seen_ref,
    gin_ref,
    gqkv_ref,
    gwo_ref,
    normed_ref,
    normed_t_ref,
    mask_ref,
    acc_ref,
    dproj_ref,
    att_ref,
):
    step = pl.program_id(0)
    rows, width = x_ref.shape
    gw = group * head_size

    @pl.when(step == 0)
    def _():
        values = x_ref[...].astype(jnp.float32)
        inv = lax.rsqrt(jnp.mean(values * values, axis=-1, keepdims=True) + epsilon)
        normed = values * inv * gain_ref[...]
        normed_ref[...] = normed.astype(jnp.bfloat16)
        normed_t_ref[...] = normed.T.astype(jnp.bfloat16)
        same = cohort_col_ref[...] == cohort_row_ref[...]
        diagonal = lax.broadcasted_iota(jnp.int32, (rows, rows), 0) == lax.broadcasted_iota(
            jnp.int32, (rows, rows), 1
        )
        seen = jnp.broadcast_to(seen_ref[...], (rows, rows)) == 1
        mask_ref[...] = jnp.where(same & (seen | diagonal), 1.0, 0.0)
        acc_ref[...] = jnp.zeros_like(acc_ref)

    normed = normed_ref[...]
    q_raw = dot(normed, wq_ref[...], ((1,), (0,)))
    k_raw = dot(normed, wk_ref[...], ((1,), (0,)))
    v_half = dot(normed, wv_ref[...], ((1,), (0,))).astype(jnp.bfloat16)
    da_half = dot(dy_ref[...], wo_ref[...], ((1,), (1,))).astype(jnp.bfloat16)
    for h in range(group):
        lanes = slice(h * head_size, (h + 1) * head_size)
        q = q_raw[:, lanes]
        k = k_raw[:, lanes]
        v = v_half[:, lanes]
        da = da_half[:, lanes]
        q_inv = lax.rsqrt(jnp.mean(q * q, axis=-1, keepdims=True) + epsilon)
        k_inv = lax.rsqrt(jnp.mean(k * k, axis=-1, keepdims=True) + epsilon)
        q_unit = q * q_inv
        k_unit = k * k_inv
        q_half = q_unit.astype(jnp.bfloat16)
        k_half = k_unit.astype(jnp.bfloat16)
        k_t = k_unit.T.astype(jnp.bfloat16)
        v_t = v.astype(jnp.float32).T.astype(jnp.bfloat16)
        scale = sharp_ref[step * group + h] / head_size
        scores = dot(k_half, q_half, ((1,), (1,)))
        grad_probs = dot(v, da, ((1,), (1,)))
        weights = jnp.exp2(scores * (scale * log2e)) * mask_ref[...]
        probs = weights * (1.0 / jnp.sum(weights, axis=0, keepdims=True))
        probs_half = probs.astype(jnp.bfloat16)
        att_t = dot(v_t, probs_half, ((1,), (0,)))
        grad_v = dot(probs_half, da, ((1,), (0,)))
        row_dot = jnp.sum(grad_probs * probs, axis=0, keepdims=True)
        grad_scores = (probs * (grad_probs - row_dot)).astype(jnp.bfloat16)
        dq = dot(k_t, grad_scores, ((1,), (0,))).T * scale
        dk = dot(grad_scores, q_half, ((1,), (0,))) * scale
        dq = q_inv * (dq - q_unit * jnp.mean(dq * q_unit, axis=-1, keepdims=True))
        dk = k_inv * (dk - k_unit * jnp.mean(dk * k_unit, axis=-1, keepdims=True))
        base = h * head_size
        dproj_ref[:, base : base + head_size] = dq.astype(jnp.bfloat16)
        dproj_ref[:, gw + base : gw + base + head_size] = dk.astype(jnp.bfloat16)
        dproj_ref[:, 2 * gw + base : 2 * gw + base + head_size] = grad_v.astype(jnp.bfloat16)
        att_ref[base : base + head_size, :] = att_t.astype(jnp.bfloat16)
    gwo_ref[...] = dot(att_ref[...], dy_ref[...], ((1,), (0,))).astype(jnp.bfloat16)
    gqkv_ref[0] = dot(normed_t_ref[...], dproj_ref[...], ((1,), (0,))).astype(jnp.bfloat16)
    acc_ref[...] += (
        dot(dproj_ref[:, :gw], wq_ref[...], ((1,), (1,)))
        + dot(dproj_ref[:, gw : 2 * gw], wk_ref[...], ((1,), (1,)))
        + dot(dproj_ref[:, 2 * gw :], wv_ref[...], ((1,), (1,)))
    )

    @pl.when(step == pl.num_programs(0) - 1)
    def _():
        values = x_ref[...].astype(jnp.float32)
        inv = lax.rsqrt(jnp.mean(values * values, axis=-1, keepdims=True) + epsilon)
        unit = values * inv
        shaped = acc_ref[...] * gain_ref[...]
        result = dy_ref[...].astype(jnp.float32) + inv * (
            shaped - unit * jnp.mean(shaped * unit, axis=-1, keepdims=True)
        )
        gin_ref[...] = result.astype(jnp.bfloat16)


def patch_grads(x, dy, norm_gain, w_qkv, w_out, sharpness, cohort_ids, seen):
    rows, width = x.shape
    heads = sharpness.shape[0]
    head_size = width // heads
    group = math.gcd(heads, 2)
    steps = heads // group
    gw = group * head_size
    whole = lambda shape: pl.BlockSpec(shape, lambda g: (0,) * len(shape))
    return pl.pallas_call(
        functools.partial(compute_kernel, head_size, group),
        grid=(steps,),
        in_specs=[
            pl.BlockSpec(memory_space=pltpu.SMEM),
            whole((rows, width)),
            whole((rows, width)),
            whole((1, width)),
            pl.BlockSpec((width, gw), lambda g: (0, g)),
            pl.BlockSpec((width, gw), lambda g: (0, steps + g)),
            pl.BlockSpec((width, gw), lambda g: (0, 2 * steps + g)),
            pl.BlockSpec((gw, width), lambda g: (g, 0)),
            whole((rows, 1)),
            whole((1, rows)),
            whole((rows, 1)),
        ],
        out_specs=[
            whole((rows, width)),
            pl.BlockSpec((1, width, 3 * gw), lambda g: (g, 0, 0)),
            pl.BlockSpec((gw, width), lambda g: (g, 0)),
        ],
        out_shape=[
            jax.ShapeDtypeStruct((rows, width), jnp.bfloat16),
            jax.ShapeDtypeStruct((steps, width, 3 * gw), jnp.bfloat16),
            jax.ShapeDtypeStruct((width, width), jnp.bfloat16),
        ],
        scratch_shapes=[
            pltpu.VMEM((rows, width), jnp.bfloat16),
            pltpu.VMEM((width, rows), jnp.bfloat16),
            pltpu.VMEM((rows, rows), jnp.float32),
            pltpu.VMEM((rows, width), jnp.float32),
            pltpu.VMEM((rows, 3 * gw), jnp.bfloat16),
            pltpu.VMEM((gw, rows), jnp.bfloat16),
        ],
        compiler_params=pltpu.CompilerParams(vmem_limit_bytes=60 * 1024 * 1024),
    )(
        sharpness,
        x,
        dy,
        norm_gain[None, :],
        w_qkv,
        w_qkv,
        w_qkv,
        w_out,
        cohort_ids[:, None],
        cohort_ids[None, :],
        seen,
    )


def scatter_kernel(n, chunks, group_cols, qkv_ref, wo_ref, out_ref, wout_ref, *scratch):
    bits = n.bit_length() - 1
    recv = scratch[:bits]
    kept = (None,) + scratch[bits : 2 * bits - 1]
    send_sem, recv_sem = scratch[2 * bits - 1 :]
    me = lax.axis_index("dev")
    bit = [(me // (1 << b)) % 2 for b in range(bits)]
    peer = [me + (1 - 2 * bit[b]) * (1 << b) for b in range(bits)]
    groups = qkv_ref.shape[0]
    cols = qkv_ref.shape[-1]
    width = wout_ref.shape[-1]

    barrier = pltpu.get_barrier_semaphore()
    for b in range(bits):
        pl.semaphore_signal(
            barrier, inc=1, device_id={"dev": peer[b]}, device_id_type=pl.DeviceIdType.MESH
        )
    pl.semaphore_wait(barrier, bits)

    def order_of(chunk):
        order = list(range(bits))
        if chunk % 2 and bits > 2:
            order[1], order[2] = order[2], order[1]
        return order

    def source(chunk, phase, side):
        order = order_of(chunk)
        left = sorted(set(range(bits)) - set(order[:phase]), reverse=True)
        picks = tuple(side if b == order[phase] else slice(None) for b in left)
        if phase:
            return kept[phase], (chunk,) + picks
        if chunk < groups:
            return qkv_ref, (chunk,) + picks
        start = (chunk - groups) * cols
        return wo_ref, picks + (slice(None), slice(start, start + cols))

    copies = {}

    def begin(chunk, phase):
        b = order_of(chunk)[phase]
        ref, index = source(chunk, phase, 1 - bit[b])
        copy = pltpu.make_async_remote_copy(
            src_ref=ref.at[index],
            dst_ref=recv[phase].at[chunk],
            send_sem=send_sem.at[chunk, phase],
            recv_sem=recv_sem.at[chunk, phase],
            device_id={"dev": peer[b]},
            device_id_type=pl.DeviceIdType.MESH,
        )
        copy.start()
        copies[chunk, phase] = copy

    def finish(chunk, phase):
        b = order_of(chunk)[phase]
        copies[chunk, phase].wait_recv()
        ref, index = source(chunk, phase, bit[b])
        total = ref[index].astype(jnp.float32) + recv[phase][chunk].astype(jnp.float32)
        if phase + 1 < bits:
            kept[phase + 1][chunk] = total.astype(jnp.bfloat16)
            begin(chunk, phase + 1)
        elif chunk < groups:
            for part in range(3):
                at = part * width + chunk * group_cols
                out_ref[:, at : at + group_cols] = total[
                    :, part * group_cols : (part + 1) * group_cols
                ]
        else:
            at = (chunk - groups) * cols
            wout_ref[:, at : at + cols] = total

    for chunk in range(chunks):
        begin(chunk, 0)
    pairs = -(-chunks // 2)
    for wave in range(pairs + bits - 1):
        for phase in reversed(range(bits)):
            pair = wave - phase
            if 0 <= pair < pairs:
                for chunk in range(2 * pair, min(2 * pair + 2, chunks)):
                    finish(chunk, phase)
    for copy in copies.values():
        copy.wait_send()


def scatter_sums(gqkv, gwo, n):
    groups, width, cols = gqkv.shape
    bits = n.bit_length() - 1
    rows = width // n
    chunks = groups + width // cols
    cube = (2,) * bits
    recv = [pltpu.VMEM((chunks,) + (2,) * (bits - 1 - p) + (rows, cols), jnp.bfloat16) for p in range(bits)]
    kept = [pltpu.VMEM((chunks,) + (2,) * (bits - p) + (rows, cols), jnp.bfloat16) for p in range(1, bits)]
    vmem = pl.BlockSpec(memory_space=pltpu.VMEM)
    return pl.pallas_call(
        functools.partial(scatter_kernel, n, chunks, cols // 3),
        in_specs=[vmem, vmem],
        out_specs=[vmem, vmem],
        out_shape=[
            jax.ShapeDtypeStruct((rows, 3 * width), jnp.float32),
            jax.ShapeDtypeStruct((rows, width), jnp.float32),
        ],
        scratch_shapes=recv
        + kept
        + [pltpu.SemaphoreType.DMA((chunks, bits)), pltpu.SemaphoreType.DMA((chunks, bits))],
        compiler_params=pltpu.CompilerParams(
            collective_id=0, has_side_effects=True, vmem_limit_bytes=40 * 1024 * 1024
        ),
        cost_estimate=pl.CostEstimate(
            flops=40_000_000_000, bytes_accessed=8 * gqkv.size, transcendentals=0
        ),
    )(gqkv.reshape((groups,) + cube + (rows, cols)), gwo.reshape(cube + (rows, width)))


def body(n, hidden_in, grad_out, norm_gain, w_qkv, w_out, sharpness, cohort_ids, observed):
    width = hidden_in.shape[-1]
    x = lax.all_to_all(hidden_in, "dev", split_axis=1, concat_axis=0, tiled=True)
    dy = lax.all_to_all(grad_out, "dev", split_axis=1, concat_axis=0, tiled=True)
    campaigns, patches, _ = x.shape
    gin, gqkv, gwo = [], 0.0, 0.0
    for p in range(patches):
        a, b, c = patch_grads(
            x[:, p], dy[:, p], norm_gain, w_qkv, w_out, sharpness, cohort_ids, observed[:, p : p + 1]
        )
        gin.append(a.reshape(n, campaigns // n, width))
        gqkv, gwo = (b, c) if p == 0 else (gqkv + b, gwo + c)
    gin = gin[0] if patches == 1 else jnp.stack(gin, axis=1).reshape(n * patches, campaigns // n, width)
    grad_in = lax.all_to_all(gin, "dev", split_axis=0, concat_axis=0, tiled=True).transpose(1, 0, 2)
    grad_qkv, grad_wout = scatter_sums(gqkv, gwo, n)
    return (grad_in, grad_qkv, grad_wout)


def solution(mesh):
    in_specs = (
        P(("grp", "dev"), None, None),
        P(("grp", "dev"), None, None),
        P(),
        P(),
        P(),
        P(),
        P("grp"),
        P("grp", "dev"),
    )
    out_specs = (P(("grp", "dev"), None, None), P(("grp", "dev"), None), P(("grp", "dev"), None))
    return jax.shard_map(functools.partial(body, mesh.shape["dev"]), mesh=mesh, in_specs=in_specs, out_specs=out_specs, check_vma=False)
```

```python
import functools
import math

import jax
import jax.numpy as jnp
from jax import lax
from jax.experimental import pallas as pl
from jax.experimental.pallas import tpu as pltpu
from jax.sharding import PartitionSpec as P


epsilon = 1e-06
log2e = math.log2(math.e)


def dot(left, right, dims):
    return lax.dot_general(left, right, ((dims[0], dims[1]), ((), ())), preferred_element_type=jnp.float32)


def forward_kernel(
    head_size,
    group,
    sharp_ref,
    x_ref,
    gain_ref,
    wq_ref,
    wk_ref,
    wv_ref,
    cohort_col_ref,
    cohort_row_ref,
    seen_ref,
    normed_t_ref,
    q_ref,
    k_ref,
    v_ref,
    inv_ref,
    probs_ref,
    att_ref,
    normed_ref,
    mask_ref,
):
    step = pl.program_id(0)
    rows, _ = x_ref.shape

    @pl.when(step == 0)
    def _():
        values = x_ref[...].astype(jnp.float32)
        inv = lax.rsqrt(jnp.mean(values * values, axis=-1, keepdims=True) + epsilon)
        normed = values * inv * gain_ref[...]
        normed_ref[...] = normed.astype(jnp.bfloat16)
        normed_t_ref[...] = normed.T.astype(jnp.bfloat16)
        same = cohort_col_ref[...] == cohort_row_ref[...]
        diagonal = lax.broadcasted_iota(jnp.int32, (rows, rows), 0) == lax.broadcasted_iota(
            jnp.int32, (rows, rows), 1
        )
        seen = jnp.broadcast_to(seen_ref[...], (rows, rows)) == 1
        mask_ref[...] = jnp.where(same & (seen | diagonal), 1.0, 0.0)

    normed = normed_ref[...]
    q_raw = dot(normed, wq_ref[...], ((1,), (0,)))
    k_raw = dot(normed, wk_ref[...], ((1,), (0,)))
    v_raw = dot(normed, wv_ref[...], ((1,), (0,)))
    v_ref[...] = v_raw.astype(jnp.bfloat16)
    for h in range(group):
        base = h * head_size
        lanes = slice(base, base + head_size)
        q = q_raw[:, lanes]
        k = k_raw[:, lanes]
        v_t = v_raw[:, lanes].T.astype(jnp.bfloat16)
        q_inv = lax.rsqrt(jnp.mean(q * q, axis=-1, keepdims=True) + epsilon)
        k_inv = lax.rsqrt(jnp.mean(k * k, axis=-1, keepdims=True) + epsilon)
        q_half = (q * q_inv).astype(jnp.bfloat16)
        k_half = (k * k_inv).astype(jnp.bfloat16)
        q_ref[:, lanes] = q_half
        k_ref[:, lanes] = k_half
        inv_ref[0, :, h : h + 1] = q_inv
        inv_ref[0, :, group + h : group + h + 1] = k_inv
        scale = sharp_ref[step * group + h] / head_size
        scores = dot(k_half, q_half, ((1,), (1,)))
        weights = jnp.exp2(scores * (scale * log2e)) * mask_ref[...]
        probs = weights * (1.0 / jnp.sum(weights, axis=0, keepdims=True))
        probs_half = probs.astype(jnp.bfloat16)
        probs_ref[h] = probs_half
        att_ref[base : base + head_size, :] = dot(v_t, probs_half, ((1,), (0,))).astype(jnp.bfloat16)


def backward_kernel(
    head_size,
    group,
    sharp_ref,
    x_ref,
    dy_ref,
    gain_ref,
    wq_ref,
    wk_ref,
    wv_ref,
    wo_ref,
    q_ref,
    k_ref,
    v_ref,
    inv_ref,
    probs_ref,
    gin_ref,
    dproj_ref,
    acc_ref,
):
    step = pl.program_id(0)
    gw = group * head_size
    da_half = dot(dy_ref[...], wo_ref[...], ((1,), (1,))).astype(jnp.bfloat16)
    for h in range(group):
        base = h * head_size
        lanes = slice(base, base + head_size)
        q_half = q_ref[:, lanes]
        k_half = k_ref[:, lanes]
        q_unit = q_half.astype(jnp.float32)
        k_unit = k_half.astype(jnp.float32)
        da = da_half[:, lanes]
        k_t = k_unit.T.astype(jnp.bfloat16)
        q_inv = inv_ref[0, :, h : h + 1]
        k_inv = inv_ref[0, :, group + h : group + h + 1]
        scale = sharp_ref[step * group + h] / head_size
        grad_probs = dot(v_ref[:, lanes], da, ((1,), (1,)))
        probs_half = probs_ref[h]
        probs = probs_half.astype(jnp.float32)
        grad_v = dot(probs_half, da, ((1,), (0,)))
        row_dot = jnp.sum(grad_probs * probs, axis=0, keepdims=True)
        grad_scores = (probs * (grad_probs - row_dot)).astype(jnp.bfloat16)
        dq = dot(k_t, grad_scores, ((1,), (0,))).T * scale
        dk = dot(grad_scores, q_half, ((1,), (0,))) * scale
        dq = q_inv * (dq - q_unit * jnp.mean(dq * q_unit, axis=-1, keepdims=True))
        dk = k_inv * (dk - k_unit * jnp.mean(dk * k_unit, axis=-1, keepdims=True))
        dproj_ref[:, base : base + head_size] = dq.astype(jnp.bfloat16)
        dproj_ref[:, gw + base : gw + base + head_size] = dk.astype(jnp.bfloat16)
        dproj_ref[:, 2 * gw + base : 2 * gw + base + head_size] = grad_v.astype(jnp.bfloat16)
    term = (
        dot(dproj_ref[:, :gw], wq_ref[...], ((1,), (1,)))
        + dot(dproj_ref[:, gw : 2 * gw], wk_ref[...], ((1,), (1,)))
        + dot(dproj_ref[:, 2 * gw :], wv_ref[...], ((1,), (1,)))
    )

    @pl.when(step == 0)
    def _():
        acc_ref[...] = term

    @pl.when(step > 0)
    def _():
        acc_ref[...] += term

    @pl.when(step == pl.num_programs(0) - 1)
    def _():
        values = x_ref[...].astype(jnp.float32)
        inv = lax.rsqrt(jnp.mean(values * values, axis=-1, keepdims=True) + epsilon)
        unit = values * inv
        shaped = acc_ref[...] * gain_ref[...]
        result = dy_ref[...].astype(jnp.float32) + inv * (
            shaped - unit * jnp.mean(shaped * unit, axis=-1, keepdims=True)
        )
        gin_ref[...] = result.astype(jnp.bfloat16)


def weights_kernel(normed_t_ref, att_ref, dproj_ref, dy_ref, gqkv_ref, gwo_ref):
    gqkv_ref[0] = dot(normed_t_ref[...], dproj_ref[...], ((1,), (0,))).astype(jnp.bfloat16)
    gwo_ref[...] = dot(att_ref[...], dy_ref[...], ((1,), (0,))).astype(jnp.bfloat16)


def patch_grads(x, dy, norm_gain, w_qkv, w_out, sharpness, cohort_ids, seen):
    rows, width = x.shape
    heads = sharpness.shape[0]
    head_size = width // heads
    group = math.gcd(heads, 2)
    steps = heads // group
    gw = group * head_size
    half = jnp.bfloat16
    whole = lambda shape: pl.BlockSpec(shape, lambda g: (0,) * len(shape))
    cols = lambda n: pl.BlockSpec((rows, n), lambda g: (0, g))
    lines = lambda n: pl.BlockSpec((gw, n), lambda g: (g, 0))
    smem = pl.BlockSpec(memory_space=pltpu.SMEM)
    weights = [
        pl.BlockSpec((width, gw), lambda g: (0, g)),
        pl.BlockSpec((width, gw), lambda g: (0, steps + g)),
        pl.BlockSpec((width, gw), lambda g: (0, 2 * steps + g)),
    ]
    invs = pl.BlockSpec((1, rows, 2 * group), lambda g: (g, 0, 0))
    probs_spec = pl.BlockSpec((group, rows, rows), lambda g: (g, 0, 0))
    params = pltpu.CompilerParams(vmem_limit_bytes=60 * 1024 * 1024)

    def cost(flops):
        return pl.CostEstimate(flops=flops, bytes_accessed=rows * width * 20, transcendentals=0)

    forward = pl.pallas_call(
        functools.partial(forward_kernel, head_size, group),
        grid=(steps,),
        in_specs=[smem, whole((rows, width)), whole((1, width))]
        + weights
        + [whole((rows, 1)), whole((1, rows)), whole((rows, 1))],
        out_specs=[whole((width, rows)), cols(gw), cols(gw), cols(gw), invs, probs_spec, lines(rows)],
        out_shape=[
            jax.ShapeDtypeStruct((width, rows), half),
            jax.ShapeDtypeStruct((rows, width), half),
            jax.ShapeDtypeStruct((rows, width), half),
            jax.ShapeDtypeStruct((rows, width), half),
            jax.ShapeDtypeStruct((steps, rows, 2 * group), jnp.float32),
            jax.ShapeDtypeStruct((heads, rows, rows), half),
            jax.ShapeDtypeStruct((width, rows), half),
        ],
        scratch_shapes=[
            pltpu.VMEM((rows, width), half),
            pltpu.VMEM((rows, rows), jnp.float32),
        ],
        compiler_params=params,
        cost_estimate=cost(40_000_000_000),
    )
    normed_t, q, k, v, inv, probs, att = forward(
        sharpness,
        x,
        norm_gain[None, :],
        w_qkv,
        w_qkv,
        w_qkv,
        cohort_ids[:, None],
        cohort_ids[None, :],
        seen,
    )
    gin, dproj = pl.pallas_call(
        functools.partial(backward_kernel, head_size, group),
        grid=(steps,),
        in_specs=[smem, whole((rows, width)), whole((rows, width)), whole((1, width))]
        + weights
        + [lines(width), cols(gw), cols(gw), cols(gw), invs, probs_spec],
        out_specs=[whole((rows, width)), cols(3 * gw)],
        out_shape=[
            jax.ShapeDtypeStruct((rows, width), half),
            jax.ShapeDtypeStruct((rows, 3 * width), half),
        ],
        scratch_shapes=[pltpu.VMEM((rows, width), jnp.float32)],
        compiler_params=params,
        cost_estimate=cost(25_000_000_000),
    )(sharpness, x, dy, norm_gain[None, :], w_qkv, w_qkv, w_qkv, w_out, q, k, v, inv, probs)
    gqkv, gwo = pl.pallas_call(
        weights_kernel,
        grid=(steps,),
        in_specs=[whole((width, rows)), lines(rows), cols(3 * gw), whole((rows, width))],
        out_specs=[pl.BlockSpec((1, width, 3 * gw), lambda g: (g, 0, 0)), lines(width)],
        out_shape=[
            jax.ShapeDtypeStruct((steps, width, 3 * gw), half),
            jax.ShapeDtypeStruct((width, width), half),
        ],
        compiler_params=params,
        cost_estimate=cost(8_000_000_000),
    )(normed_t, att, dproj, dy)
    return gin, gqkv, gwo


def scatter_kernel(n, chunks, group_cols, qkv_ref, wo_ref, out_ref, wout_ref, *scratch):
    bits = n.bit_length() - 1
    recv = scratch[:bits]
    kept = (None,) + scratch[bits : 2 * bits - 1]
    send_sem, recv_sem = scratch[2 * bits - 1 :]
    me = lax.axis_index("dev")
    bit = [(me // (1 << b)) % 2 for b in range(bits)]
    peer = [me + (1 - 2 * bit[b]) * (1 << b) for b in range(bits)]
    groups = qkv_ref.shape[0]
    cols = qkv_ref.shape[-1]
    width = wout_ref.shape[-1]

    barrier = pltpu.get_barrier_semaphore()
    for b in range(bits):
        pl.semaphore_signal(
            barrier, inc=1, device_id={"dev": peer[b]}, device_id_type=pl.DeviceIdType.MESH
        )
    pl.semaphore_wait(barrier, bits)

    def order_of(chunk):
        order = list(range(bits))
        if chunk % 2 and bits > 2:
            order[1], order[2] = order[2], order[1]
        return order

    def source(chunk, phase, side):
        order = order_of(chunk)
        left = sorted(set(range(bits)) - set(order[:phase]), reverse=True)
        picks = tuple(side if b == order[phase] else slice(None) for b in left)
        if phase:
            return kept[phase], (chunk,) + picks
        if chunk < groups:
            return qkv_ref, (chunk,) + picks
        start = (chunk - groups) * cols
        return wo_ref, picks + (slice(None), slice(start, start + cols))

    copies = {}

    def begin(chunk, phase):
        b = order_of(chunk)[phase]
        ref, index = source(chunk, phase, 1 - bit[b])
        copy = pltpu.make_async_remote_copy(
            src_ref=ref.at[index],
            dst_ref=recv[phase].at[chunk],
            send_sem=send_sem.at[chunk, phase],
            recv_sem=recv_sem.at[chunk, phase],
            device_id={"dev": peer[b]},
            device_id_type=pl.DeviceIdType.MESH,
        )
        copy.start()
        copies[chunk, phase] = copy

    def finish(chunk, phase):
        b = order_of(chunk)[phase]
        copies[chunk, phase].wait_recv()
        ref, index = source(chunk, phase, bit[b])
        total = ref[index].astype(jnp.float32) + recv[phase][chunk].astype(jnp.float32)
        if phase + 1 < bits:
            kept[phase + 1][chunk] = total.astype(jnp.bfloat16)
            begin(chunk, phase + 1)
        elif chunk < groups:
            for part in range(3):
                at = part * width + chunk * group_cols
                out_ref[:, at : at + group_cols] = total[
                    :, part * group_cols : (part + 1) * group_cols
                ]
        else:
            at = (chunk - groups) * cols
            wout_ref[:, at : at + cols] = total

    for chunk in range(chunks):
        begin(chunk, 0)
    pairs = -(-chunks // 2)
    for wave in range(pairs + bits - 1):
        for phase in reversed(range(bits)):
            pair = wave - phase
            if 0 <= pair < pairs:
                for chunk in range(2 * pair, min(2 * pair + 2, chunks)):
                    finish(chunk, phase)
    for copy in copies.values():
        copy.wait_send()


def scatter_sums(gqkv, gwo, n):
    groups, width, cols = gqkv.shape
    bits = n.bit_length() - 1
    rows = width // n
    chunks = groups + width // cols
    cube = (2,) * bits
    recv = [pltpu.VMEM((chunks,) + (2,) * (bits - 1 - p) + (rows, cols), jnp.bfloat16) for p in range(bits)]
    kept = [pltpu.VMEM((chunks,) + (2,) * (bits - p) + (rows, cols), jnp.bfloat16) for p in range(1, bits)]
    vmem = pl.BlockSpec(memory_space=pltpu.VMEM)
    return pl.pallas_call(
        functools.partial(scatter_kernel, n, chunks, cols // 3),
        in_specs=[vmem, vmem],
        out_specs=[vmem, vmem],
        out_shape=[
            jax.ShapeDtypeStruct((rows, 3 * width), jnp.float32),
            jax.ShapeDtypeStruct((rows, width), jnp.float32),
        ],
        scratch_shapes=recv
        + kept
        + [pltpu.SemaphoreType.DMA((chunks, bits)), pltpu.SemaphoreType.DMA((chunks, bits))],
        compiler_params=pltpu.CompilerParams(
            collective_id=0, has_side_effects=True, vmem_limit_bytes=40 * 1024 * 1024
        ),
        cost_estimate=pl.CostEstimate(
            flops=40_000_000_000, bytes_accessed=8 * gqkv.size, transcendentals=0
        ),
    )(gqkv.reshape((groups,) + cube + (rows, cols)), gwo.reshape(cube + (rows, width)))


def body(n, *args):
    return layer(n, *args)


def layer(n, hidden_in, grad_out, norm_gain, w_qkv, w_out, sharpness, cohort_ids, observed):
    width = hidden_in.shape[-1]
    x = lax.all_to_all(hidden_in, "dev", split_axis=1, concat_axis=0, tiled=True)
    dy = lax.all_to_all(grad_out, "dev", split_axis=1, concat_axis=0, tiled=True)
    campaigns, patches, _ = x.shape
    gin, gqkv, gwo = [], 0.0, 0.0
    for p in range(patches):
        a, b, c = patch_grads(
            x[:, p], dy[:, p], norm_gain, w_qkv, w_out, sharpness, cohort_ids, observed[:, p : p + 1]
        )
        gin.append(a.reshape(n, campaigns // n, width))
        gqkv, gwo = (b, c) if p == 0 else (gqkv + b, gwo + c)
    gin = gin[0] if patches == 1 else jnp.stack(gin, axis=1).reshape(n * patches, campaigns // n, width)
    grad_in = lax.all_to_all(gin, "dev", split_axis=0, concat_axis=0, tiled=True).transpose(1, 0, 2)
    grad_qkv, grad_wout = scatter_sums(gqkv, gwo, n)
    return (grad_in, grad_qkv, grad_wout)


def solution(mesh):
    in_specs = (
        P(("grp", "dev"), None, None),
        P(("grp", "dev"), None, None),
        P(),
        P(),
        P(),
        P(),
        P("grp"),
        P("grp", "dev"),
    )
    out_specs = (P(("grp", "dev"), None, None), P(("grp", "dev"), None), P(("grp", "dev"), None))
    return jax.shard_map(functools.partial(body, mesh.shape["dev"]), mesh=mesh, in_specs=in_specs, out_specs=out_specs, check_vma=False)
```

```python
import functools
import math

import jax
import jax.numpy as jnp
from jax import lax
from jax.experimental import pallas as pl
from jax.experimental.pallas import tpu as pltpu
from jax.sharding import PartitionSpec as P


epsilon = 1e-06
log2e = math.log2(math.e)


def dot(left, right, dims):
    return lax.dot_general(left, right, ((dims[0], dims[1]), ((), ())), preferred_element_type=jnp.float32)


def forward_kernel(
    head_size,
    group,
    sharp_ref,
    x_ref,
    gain_ref,
    wq_ref,
    wk_ref,
    wv_ref,
    cohort_col_ref,
    cohort_row_ref,
    seen_ref,
    normed_t_ref,
    q_ref,
    k_ref,
    k_t_ref,
    v_ref,
    inv_ref,
    probs_ref,
    att_ref,
    normed_ref,
    mask_ref,
):
    step = pl.program_id(0)
    rows, _ = x_ref.shape

    @pl.when(step == 0)
    def _():
        values = x_ref[...].astype(jnp.float32)
        inv = lax.rsqrt(jnp.mean(values * values, axis=-1, keepdims=True) + epsilon)
        normed = values * inv * gain_ref[...]
        normed_ref[...] = normed.astype(jnp.bfloat16)
        normed_t_ref[...] = normed.T.astype(jnp.bfloat16)
        same = cohort_col_ref[...] == cohort_row_ref[...]
        diagonal = lax.broadcasted_iota(jnp.int32, (rows, rows), 0) == lax.broadcasted_iota(
            jnp.int32, (rows, rows), 1
        )
        seen = jnp.broadcast_to(seen_ref[...], (rows, rows)) == 1
        mask_ref[...] = jnp.where(same & (seen | diagonal), 1.0, 0.0)

    normed = normed_ref[...]
    q_raw = dot(normed, wq_ref[...], ((1,), (0,)))
    k_raw = dot(normed, wk_ref[...], ((1,), (0,)))
    v_raw = dot(normed, wv_ref[...], ((1,), (0,)))
    v_ref[...] = v_raw.astype(jnp.bfloat16)
    for h in range(group):
        base = h * head_size
        lanes = slice(base, base + head_size)
        q = q_raw[:, lanes]
        k = k_raw[:, lanes]
        v_t = v_raw[:, lanes].T.astype(jnp.bfloat16)
        q_inv = lax.rsqrt(jnp.mean(q * q, axis=-1, keepdims=True) + epsilon)
        k_inv = lax.rsqrt(jnp.mean(k * k, axis=-1, keepdims=True) + epsilon)
        q_half = (q * q_inv).astype(jnp.bfloat16)
        k_unit = k * k_inv
        k_half = k_unit.astype(jnp.bfloat16)
        k_t_ref[lanes, :] = k_unit.T.astype(jnp.bfloat16)
        q_ref[:, lanes] = q_half
        k_ref[:, lanes] = k_half
        inv_ref[0, :, h : h + 1] = q_inv
        inv_ref[0, :, group + h : group + h + 1] = k_inv
        scale = sharp_ref[step * group + h] / head_size
        scores = dot(k_half, q_half, ((1,), (1,)))
        weights = jnp.exp2(scores * (scale * log2e)) * mask_ref[...]
        probs = weights * (1.0 / jnp.sum(weights, axis=0, keepdims=True))
        probs_half = probs.astype(jnp.bfloat16)
        probs_ref[h] = probs_half
        att_ref[base : base + head_size, :] = dot(v_t, probs_half, ((1,), (0,))).astype(jnp.bfloat16)


def backward_kernel(
    head_size,
    group,
    sharp_ref,
    x_ref,
    dy_ref,
    gain_ref,
    wqkv_t_ref,
    wo_t_ref,
    q_ref,
    k_ref,
    k_t_ref,
    v_ref,
    inv_ref,
    probs_ref,
    gin_ref,
    dproj_ref,
):
    step = pl.program_id(0)
    gw = group * head_size
    width = x_ref.shape[1]
    da_half = dot(dy_ref[...], wo_t_ref[...], ((1,), (0,))).astype(jnp.bfloat16)
    parts = ([], [], [])
    for h in range(group):
        base = h * head_size
        lanes = slice(base, base + head_size)
        q_half = q_ref[:, lanes]
        q_unit = q_half.astype(jnp.float32)
        k_unit = k_ref[:, lanes].astype(jnp.float32)
        da = da_half[:, lanes]
        q_inv = inv_ref[0, :, h : h + 1]
        k_inv = inv_ref[0, :, group + h : group + h + 1]
        scale = sharp_ref[step * group + h] / head_size
        grad_probs = dot(v_ref[:, lanes], da, ((1,), (1,)))
        probs_half = probs_ref[h]
        probs = probs_half.astype(jnp.float32)
        grad_v = dot(probs_half, da, ((1,), (0,)))
        row_dot = jnp.sum(grad_probs * probs, axis=0, keepdims=True)
        grad_scores = (probs * (grad_probs - row_dot)).astype(jnp.bfloat16)
        dq = dot(k_t_ref[lanes, :], grad_scores, ((1,), (0,))).T * scale
        dk = dot(grad_scores, q_half, ((1,), (0,))) * scale
        dq = q_inv * (dq - q_unit * jnp.mean(dq * q_unit, axis=-1, keepdims=True))
        dk = k_inv * (dk - k_unit * jnp.mean(dk * k_unit, axis=-1, keepdims=True))
        for part, value in zip(parts, (dq, dk, grad_v)):
            part.append(value.astype(jnp.bfloat16))
    for at, part in enumerate(parts):
        start = pl.multiple_of(at * width + step * gw, gw)
        dproj_ref[:, pl.ds(start, gw)] = jnp.concatenate(part, axis=1)

    @pl.when(step == pl.num_programs(0) - 1)
    def _():
        values = x_ref[...].astype(jnp.float32)
        inv = lax.rsqrt(jnp.mean(values * values, axis=-1, keepdims=True) + epsilon)
        unit = values * inv
        shaped = dot(dproj_ref[...], wqkv_t_ref[...], ((1,), (0,))) * gain_ref[...]
        result = dy_ref[...].astype(jnp.float32) + inv * (
            shaped - unit * jnp.mean(shaped * unit, axis=-1, keepdims=True)
        )
        gin_ref[...] = result.astype(jnp.bfloat16)


def weights_kernel(normed_t_ref, att_ref, dq_ref, dk_ref, dv_ref, dy_ref, gqkv_ref, gwo_ref):
    dproj = jnp.concatenate([dq_ref[...], dk_ref[...], dv_ref[...]], axis=1)
    gqkv_ref[0] = dot(normed_t_ref[...], dproj, ((1,), (0,))).astype(jnp.bfloat16)
    gwo_ref[...] = dot(att_ref[...], dy_ref[...], ((1,), (0,))).astype(jnp.bfloat16)


def patch_grads(x, dy, norm_gain, w_qkv, w_out, sharpness, cohort_ids, seen):
    rows, width = x.shape
    heads = sharpness.shape[0]
    head_size = width // heads
    group = math.gcd(heads, 2)
    steps = heads // group
    gw = group * head_size
    half = jnp.bfloat16
    whole = lambda shape: pl.BlockSpec(shape, lambda g: (0,) * len(shape))
    cols = lambda n: pl.BlockSpec((rows, n), lambda g: (0, g))
    lines = lambda n: pl.BlockSpec((gw, n), lambda g: (g, 0))
    smem = pl.BlockSpec(memory_space=pltpu.SMEM)
    weights = [
        pl.BlockSpec((width, gw), lambda g: (0, g)),
        pl.BlockSpec((width, gw), lambda g: (0, steps + g)),
        pl.BlockSpec((width, gw), lambda g: (0, 2 * steps + g)),
    ]
    invs = pl.BlockSpec((1, rows, 2 * group), lambda g: (g, 0, 0))
    probs_spec = pl.BlockSpec((group, rows, rows), lambda g: (g, 0, 0))
    w_qkv_t, w_out_t = w_qkv.T, w_out.T
    params = pltpu.CompilerParams(vmem_limit_bytes=60 * 1024 * 1024)

    def cost(flops):
        return pl.CostEstimate(flops=flops, bytes_accessed=rows * width * 20, transcendentals=0)

    forward = pl.pallas_call(
        functools.partial(forward_kernel, head_size, group),
        grid=(steps,),
        in_specs=[smem, whole((rows, width)), whole((1, width))]
        + weights
        + [whole((rows, 1)), whole((1, rows)), whole((rows, 1))],
        out_specs=[whole((width, rows)), cols(gw), cols(gw), lines(rows), cols(gw), invs, probs_spec, lines(rows)],
        out_shape=[
            jax.ShapeDtypeStruct((width, rows), half),
            jax.ShapeDtypeStruct((rows, width), half),
            jax.ShapeDtypeStruct((rows, width), half),
            jax.ShapeDtypeStruct((width, rows), half),
            jax.ShapeDtypeStruct((rows, width), half),
            jax.ShapeDtypeStruct((steps, rows, 2 * group), jnp.float32),
            jax.ShapeDtypeStruct((heads, rows, rows), half),
            jax.ShapeDtypeStruct((width, rows), half),
        ],
        scratch_shapes=[
            pltpu.VMEM((rows, width), half),
            pltpu.VMEM((rows, rows), jnp.float32),
        ],
        compiler_params=params,
        cost_estimate=cost(40_000_000_000),
    )
    normed_t, q, k, k_t, v, inv, probs, att = forward(
        sharpness,
        x,
        norm_gain[None, :],
        w_qkv,
        w_qkv,
        w_qkv,
        cohort_ids[:, None],
        cohort_ids[None, :],
        seen,
    )
    gin, dproj = pl.pallas_call(
        functools.partial(backward_kernel, head_size, group),
        grid=(steps,),
        in_specs=[
            smem,
            whole((rows, width)),
            whole((rows, width)),
            whole((1, width)),
            whole((3 * width, width)),
            pl.BlockSpec((width, gw), lambda g: (0, g)),
            cols(gw),
            cols(gw),
            lines(rows),
            cols(gw),
            invs,
            probs_spec,
        ],
        out_specs=[whole((rows, width)), whole((rows, 3 * width))],
        out_shape=[
            jax.ShapeDtypeStruct((rows, width), half),
            jax.ShapeDtypeStruct((rows, 3 * width), half),
        ],
        compiler_params=params,
        cost_estimate=cost(25_000_000_000),
    )(sharpness, x, dy, norm_gain[None, :], w_qkv_t, w_out_t, q, k, k_t, v, inv, probs)
    gqkv, gwo = pl.pallas_call(
        weights_kernel,
        grid=(steps,),
        in_specs=[
            whole((width, rows)),
            lines(rows),
            cols(gw),
            pl.BlockSpec((rows, gw), lambda g: (0, steps + g)),
            pl.BlockSpec((rows, gw), lambda g: (0, 2 * steps + g)),
            whole((rows, width)),
        ],
        out_specs=[pl.BlockSpec((1, width, 3 * gw), lambda g: (g, 0, 0)), lines(width)],
        out_shape=[
            jax.ShapeDtypeStruct((steps, width, 3 * gw), half),
            jax.ShapeDtypeStruct((width, width), half),
        ],
        compiler_params=params,
        cost_estimate=cost(8_000_000_000),
    )(normed_t, att, dproj, dproj, dproj, dy)
    return gin, gqkv, gwo


def scatter_kernel(n, chunks, group_cols, qkv_ref, wo_ref, out_ref, wout_ref, *scratch):
    bits = n.bit_length() - 1
    recv = scratch[:bits]
    kept = (None,) + scratch[bits : 2 * bits - 1]
    send_sem, recv_sem = scratch[2 * bits - 1 :]
    me = lax.axis_index("dev")
    bit = [(me // (1 << b)) % 2 for b in range(bits)]
    peer = [me + (1 - 2 * bit[b]) * (1 << b) for b in range(bits)]
    groups = qkv_ref.shape[0]
    cols = qkv_ref.shape[-1]
    width = wout_ref.shape[-1]

    barrier = pltpu.get_barrier_semaphore()
    for b in range(bits):
        pl.semaphore_signal(
            barrier, inc=1, device_id={"dev": peer[b]}, device_id_type=pl.DeviceIdType.MESH
        )
    pl.semaphore_wait(barrier, bits)

    def order_of(chunk):
        order = list(range(bits))
        if chunk % 2 and bits > 2:
            order[1], order[2] = order[2], order[1]
        return order

    def source(chunk, phase, side):
        order = order_of(chunk)
        left = sorted(set(range(bits)) - set(order[:phase]), reverse=True)
        picks = tuple(side if b == order[phase] else slice(None) for b in left)
        if phase:
            return kept[phase], (chunk,) + picks
        if chunk < groups:
            return qkv_ref, (chunk,) + picks
        start = (chunk - groups) * cols
        return wo_ref, picks + (slice(None), slice(start, start + cols))

    copies = {}

    def begin(chunk, phase):
        b = order_of(chunk)[phase]
        ref, index = source(chunk, phase, 1 - bit[b])
        copy = pltpu.make_async_remote_copy(
            src_ref=ref.at[index],
            dst_ref=recv[phase].at[chunk],
            send_sem=send_sem.at[chunk, phase],
            recv_sem=recv_sem.at[chunk, phase],
            device_id={"dev": peer[b]},
            device_id_type=pl.DeviceIdType.MESH,
        )
        copy.start()
        copies[chunk, phase] = copy

    def finish(chunk, phase):
        b = order_of(chunk)[phase]
        copies[chunk, phase].wait_recv()
        ref, index = source(chunk, phase, bit[b])
        total = ref[index].astype(jnp.float32) + recv[phase][chunk].astype(jnp.float32)
        if phase + 1 < bits:
            kept[phase + 1][chunk] = total.astype(jnp.bfloat16)
            begin(chunk, phase + 1)
        elif chunk < groups:
            for part in range(3):
                at = part * width + chunk * group_cols
                out_ref[:, at : at + group_cols] = total[
                    :, part * group_cols : (part + 1) * group_cols
                ]
        else:
            at = (chunk - groups) * cols
            wout_ref[:, at : at + cols] = total

    for chunk in range(chunks):
        begin(chunk, 0)
    pairs = -(-chunks // 2)
    for wave in range(pairs + bits - 1):
        for phase in reversed(range(bits)):
            pair = wave - phase
            if 0 <= pair < pairs:
                for chunk in range(2 * pair, min(2 * pair + 2, chunks)):
                    finish(chunk, phase)
    for copy in copies.values():
        copy.wait_send()


def scatter_sums(gqkv, gwo, n):
    groups, width, cols = gqkv.shape
    bits = n.bit_length() - 1
    rows = width // n
    chunks = groups + width // cols
    cube = (2,) * bits
    recv = [pltpu.VMEM((chunks,) + (2,) * (bits - 1 - p) + (rows, cols), jnp.bfloat16) for p in range(bits)]
    kept = [pltpu.VMEM((chunks,) + (2,) * (bits - p) + (rows, cols), jnp.bfloat16) for p in range(1, bits)]
    vmem = pl.BlockSpec(memory_space=pltpu.VMEM)
    return pl.pallas_call(
        functools.partial(scatter_kernel, n, chunks, cols // 3),
        in_specs=[vmem, vmem],
        out_specs=[vmem, vmem],
        out_shape=[
            jax.ShapeDtypeStruct((rows, 3 * width), jnp.float32),
            jax.ShapeDtypeStruct((rows, width), jnp.float32),
        ],
        scratch_shapes=recv
        + kept
        + [pltpu.SemaphoreType.DMA((chunks, bits)), pltpu.SemaphoreType.DMA((chunks, bits))],
        compiler_params=pltpu.CompilerParams(
            collective_id=0, has_side_effects=True, vmem_limit_bytes=40 * 1024 * 1024
        ),
        cost_estimate=pl.CostEstimate(
            flops=40_000_000_000, bytes_accessed=8 * gqkv.size, transcendentals=0
        ),
    )(gqkv.reshape((groups,) + cube + (rows, cols)), gwo.reshape(cube + (rows, width)))


def body(n, *args):
    return layer(n, *args)


def layer(n, hidden_in, grad_out, norm_gain, w_qkv, w_out, sharpness, cohort_ids, observed):
    width = hidden_in.shape[-1]
    x = lax.all_to_all(hidden_in, "dev", split_axis=1, concat_axis=0, tiled=True)
    dy = lax.all_to_all(grad_out, "dev", split_axis=1, concat_axis=0, tiled=True)
    campaigns, patches, _ = x.shape
    gin, gqkv, gwo = [], 0.0, 0.0
    for p in range(patches):
        a, b, c = patch_grads(
            x[:, p], dy[:, p], norm_gain, w_qkv, w_out, sharpness, cohort_ids, observed[:, p : p + 1]
        )
        gin.append(a.reshape(n, campaigns // n, width))
        gqkv, gwo = (b, c) if p == 0 else (gqkv + b, gwo + c)
    gin = gin[0] if patches == 1 else jnp.stack(gin, axis=1).reshape(n * patches, campaigns // n, width)
    grad_in = lax.all_to_all(gin, "dev", split_axis=0, concat_axis=0, tiled=True).transpose(1, 0, 2)
    grad_qkv, grad_wout = scatter_sums(gqkv, gwo, n)
    return (grad_in, grad_qkv, grad_wout)


def solution(mesh):
    in_specs = (
        P(("grp", "dev"), None, None),
        P(("grp", "dev"), None, None),
        P(),
        P(),
        P(),
        P(),
        P("grp"),
        P("grp", "dev"),
    )
    out_specs = (P(("grp", "dev"), None, None), P(("grp", "dev"), None), P(("grp", "dev"), None))
    return jax.shard_map(functools.partial(body, mesh.shape["dev"]), mesh=mesh, in_specs=in_specs, out_specs=out_specs, check_vma=False)
```
